32 devices in a mesh: parts: 2 (over y), space: 4 (over z), dp: 2 (over x), chan: 2 (over core).
Axes of the slice: x: 2, y: 2, z: 4, core: 2. Of those that a mesh axis runs over, the one named last changes fastest.
Arguments:
- grad_out: bfloat16 [4, 4, 16, 16, 1024], P(('parts', 'dp'), 'space', None, None, 'chan'), parts along dimension 0, may hold values from -6 to 6
- saved_spectrum: bfloat16 [2, 4, 4, 16, 16, 1024], P(None, ('parts', 'dp'), None, 'space', None, 'chan'), parts along dimension 1, may hold values from -6 to 6
- w_first: bfloat16 [8, 2, 128, 128], P('chan'), may hold values from -0.375 to 0.375
- bias_first: bfloat16 [2, 1024], P(None, 'chan'), may hold values from -3 to 3
- w_second: bfloat16 [8, 2, 128, 128], P('chan'), may hold values from -0.375 to 0.375
Outputs:
- grad_in: bfloat16 [4, 4, 16, 16, 1024], P(('parts', 'dp'), 'space', None, None, 'chan'), parts along dimension 0
- grad_first: float32 [16, 2, 128, 128], P(('parts', 'chan'), None, ('space', 'dp')), parts along dimension 0
- grad_second: float32 [16, 2, 128, 128], P(('parts', 'chan'), None, ('space', 'dp')), parts along dimension 0
The draws below stay inside these ranges and needn't reach their ends.
There are 2 independent parts, one for each index of `parts`. The reference program is written for one: setup_inputs(seed, part) draws one part's arguments, and reference() takes and returns one part's arrays. A program takes and returns all parts, laid end to end along the dimension named above; an argument that names none is the same for every part. Nothing has to cross between parts.
All inputs are finite; a program needn't handle non-finite values.
Results may differ from the reference program's by a relative error of at most 0.013.
Values may be sent and summed in bfloat16 or wider, within the bound.
A program may use at most 64 MiB of HBM per device.

```python
import math
import jax
import jax.numpy as jnp
from jax import lax

WIDTH = 1024
BLOCK = 128
NBLOCK = 8
GY = 16
GZ = 16
GX = 4
SAMPLES = 2


def block_levels(key, extent, pieces, smallest, high):
    factor_of = 1.0
    for axis_at, parts in pieces:
        draws = jax.random.uniform(jax.random.fold_in(jax.random.fold_in(key, 6), axis_at), (parts,), jnp.float32, smallest / len(pieces), high / len(pieces))
        factor_of = factor_of * jnp.repeat(jnp.exp(draws), extent[axis_at] // parts).reshape((-1,) + (1,) * (len(extent) - 1 - axis_at))
    return factor_of


def gaussian(rng, dims, scale, reach, pieces=(), kind=jnp.bfloat16):
    entries = scale * jax.random.normal(rng, dims, jnp.float32)
    if pieces:
        entries = entries * block_levels(rng, dims, pieces, -0.22, 0.18)
    return jnp.clip(entries, -reach, reach).astype(kind)


def setup_inputs(seed: int = 0, part: int = 0) -> dict:
    arg_keys = jax.random.split(jax.random.key(seed), 6)
    part_keys = jax.random.split(jax.random.fold_in(arg_keys[5], part), 6)
    grad_out = gaussian(part_keys[0], (SAMPLES, GX, GY, GZ, WIDTH), 1.0, 6.0, ((0, 2), (1, 4), (4, 2)))
    saved_spectrum = gaussian(part_keys[1], (2, SAMPLES, GX, GY, GZ, WIDTH), 0.8, 6.0, ((1, 2), (3, 4), (5, 2)))
    w_first = gaussian(arg_keys[2], (NBLOCK, 2, BLOCK, BLOCK), (2 * BLOCK) ** -0.5, 0.375, ((0, 2),))
    bias_first = gaussian(arg_keys[3], (2, WIDTH), 0.5, 3.0, ((1, 2),))
    w_second = gaussian(arg_keys[4], (NBLOCK, 2, BLOCK, BLOCK), (2 * BLOCK) ** -0.5, 0.375, ((0, 2),))
    return dict(grad_out=grad_out, saved_spectrum=saved_spectrum, w_first=w_first, bias_first=bias_first, w_second=w_second)


inv_root_two = 1.0 / math.sqrt(2.0)
inv_root_tau = 1.0 / math.sqrt(2.0 * math.pi)

def gelu_value(values):
    return values * 0.5 * (1.0 + lax.erf(values * inv_root_two))

def gelu_slope(values):
    return 0.5 * (1.0 + lax.erf(values * inv_root_two)) + values * jnp.exp(-0.5 * values * values) * inv_root_tau

def rounded(values):
    return lax.optimization_barrier(values.astype(jnp.bfloat16)).astype(jnp.float32)

def forward_product(left, right):
    return jnp.einsum('xyzbc,bcd->xyzbd', left, right, precision=lax.Precision.HIGHEST)

def adjoint_product(left, right):
    return jnp.einsum('xyzbd,bcd->xyzbc', left, right, precision=lax.Precision.HIGHEST)

def weight_product(left, right):
    return jnp.einsum('xyzbc,xyzbd->bcd', left, right, precision=lax.Precision.HIGHEST)

def reference(grad_out, saved_spectrum, w_first, bias_first, w_second):
    samples, length_x, length_y, length_z, width = grad_out.shape
    count = w_first.shape[0]
    block = w_first.shape[2]
    cells = length_x * length_y * length_z
    norm_scale = 1.0 / math.sqrt(cells)
    grad_scale = 1.0 / math.sqrt(cells * samples)
    first_real = w_first[:, 0].astype(jnp.float32)
    first_imag = w_first[:, 1].astype(jnp.float32)
    second_real = w_second[:, 0].astype(jnp.float32)
    second_imag = w_second[:, 1].astype(jnp.float32)
    bias = bias_first.astype(jnp.float32).reshape(2, count, block)
    blocked = (length_x, length_y, length_z, count, block)

    def one_sample(totals, inputs):
        grad, saved = inputs
        partial_spec = jnp.fft.fftn(grad.astype(jnp.float32), axes=(1, 2))
        partial_spec = lax.complex(rounded(jnp.real(partial_spec)), rounded(jnp.imag(partial_spec)))
        whole = jnp.fft.fft(partial_spec, axis=0) * norm_scale
        grad_real = rounded(jnp.real(whole)).reshape(blocked)
        grad_imag = rounded(jnp.imag(whole)).reshape(blocked)
        saved_real = saved[0].astype(jnp.float32).reshape(blocked)
        saved_imag = saved[1].astype(jnp.float32).reshape(blocked)
        pre_real = forward_product(saved_real, first_real) - forward_product(saved_imag, first_imag) + bias[0]
        pre_imag = forward_product(saved_real, first_imag) + forward_product(saved_imag, first_real) + bias[1]
        act_real = rounded(gelu_value(pre_real))
        act_imag = rounded(gelu_value(pre_imag))
        back_real = adjoint_product(grad_real, second_real) + adjoint_product(grad_imag, second_imag)
        back_imag = adjoint_product(grad_imag, second_real) - adjoint_product(grad_real, second_imag)
        slope_real = rounded(back_real * gelu_slope(pre_real))
        slope_imag = rounded(back_imag * gelu_slope(pre_imag))
        input_real = adjoint_product(slope_real, first_real) + adjoint_product(slope_imag, first_imag)
        input_imag = adjoint_product(slope_imag, first_real) - adjoint_product(slope_real, first_imag)
        second_term = jnp.stack([weight_product(act_real, grad_real) + weight_product(act_imag, grad_imag), weight_product(act_real, grad_imag) - weight_product(act_imag, grad_real)], axis=1)
        first_term = jnp.stack([weight_product(saved_real, slope_real) + weight_product(saved_imag, slope_imag), weight_product(saved_real, slope_imag) - weight_product(saved_imag, slope_real)], axis=1)
        spectrum_in = lax.complex(input_real.reshape(grad.shape), input_imag.reshape(grad.shape))
        planes_back = jnp.fft.ifft(spectrum_in, axis=0) * length_x
        planes_back = lax.complex(rounded(jnp.real(planes_back)), rounded(jnp.imag(planes_back)))
        field = jnp.fft.ifftn(planes_back, axes=(1, 2)) * (length_y * length_z)
        result = (jnp.real(field) * norm_scale).astype(jnp.bfloat16)
        return ((totals[0] + first_term, totals[1] + second_term), result)
    zeros = jnp.zeros((count, 2, block, block), jnp.float32)
    totals, grad_in = lax.scan(one_sample, (zeros, zeros), (grad_out, jnp.moveaxis(saved_spectrum, 0, 1)))
    return (grad_in, totals[0] * grad_scale, totals[1] * grad_scale)
```

```python
import functools
import math

import jax
import jax.numpy as jnp
import ml_dtypes
import numpy as np
from jax import lax
from jax.experimental import pallas as pl
from jax.experimental.pallas import tpu as pltpu
from jax.sharding import PartitionSpec as P

inv_root_two = 1.0 / math.sqrt(2.0)
inv_root_tau = 1.0 / math.sqrt(2.0 * math.pi)
f32 = jnp.float32
bf16 = jnp.bfloat16
MESH = pl.DeviceIdType.MESH


def scaled_table(table):
    best = None
    for step in range(512):
        factor = 1.0 + step / 512.0
        exact = table * factor
        kept = exact.astype(ml_dtypes.bfloat16).astype(np.float64)
        fit = float((kept * table).sum() / (table * table).sum())
        error = float(((kept - fit * table) ** 2).sum() / (kept**2).sum())
        if best is None or error < best[0]:
            best = (error, fit, kept.astype(ml_dtypes.bfloat16))
    return best[1], best[2]


def plane_table(length_y, length_z, shards):
    ky = np.arange(length_y)[:, None, None, None]
    kz = np.arange(length_z)[None, :, None, None]
    y = np.arange(length_y)[None, None, :, None]
    z = np.arange(length_z)[None, None, None, :]
    angle = 2.0 * np.pi * (ky * y / length_y + kz * z / length_z)
    both = np.stack([np.cos(angle), -np.sin(angle)])
    both = np.round(both, 12)
    both = both.reshape(2, shards, length_y // shards, length_z, length_y * length_z)
    return both.transpose(1, 0, 2, 3, 4).reshape(2 * length_y * length_z, -1)


def times(value, factor):
    re, im = value
    c, s = factor.real, factor.imag
    if abs(s) < 1e-12:
        return (re, im) if abs(c - 1.0) < 1e-12 else (re * c, im * c)
    if abs(c) < 1e-12:
        if abs(s - 1.0) < 1e-12:
            return (-im, re)
        if abs(s + 1.0) < 1e-12:
            return (im, -re)
        return (-im * s, re * s)
    return (re * c - im * s, re * s + im * c)


def plus(a, b):
    return (a[0] + b[0], a[1] + b[1])


def minus(a, b):
    return (a[0] - b[0], a[1] - b[1])


def transform(values, orient):
    n = len(values)
    if n == 1:
        return values
    root = lambda k: complex(math.cos(2 * math.pi * k / n), orient * math.sin(2 * math.pi * k / n))
    if n % 2:
        out = []
        for k in range(n):
            total = values[0]
            for j in range(1, n):
                total = plus(total, times(values[j], root(k * j % n)))
            out.append(total)
        return out
    even = transform(values[0::2], orient)
    odd = transform(values[1::2], orient)
    turned = [times(odd[k], root(k)) for k in range(n // 2)]
    return [plus(even[k], turned[k]) for k in range(n // 2)] + [
        minus(even[k], turned[k]) for k in range(n // 2)
    ]


def dot(a, b, ca, cb):
    return lax.dot_general(a, b, (((ca,), (cb,)), ((), ())), preferred_element_type=f32)


def stacked(re, im):
    top = jnp.concatenate([re, im], axis=1)
    low = jnp.concatenate([-im, re], axis=1)
    return jnp.concatenate([top, low], axis=0)


def kernel(dims, x_hbm, s_hbm, w1_hbm, b_hbm, w2_hbm, t1_hbm, t2_hbm,
           gin_hbm, g1_hbm, g2_hbm,
           x_v, s_v, w1_v, b_v, w2_v, t1_v, t2_v,
           psend, precv, z_v, act, slope, gsc, dz_v, ds_v, qsend, qrecv, gin_v,
           gbuf, drecv, zsend, zrecv, g1_v, g2_v,
           in_sem, out_sem, ps_sem, pr_sem, qs_sem, qr_sem, ds_sem, dr_sem, zs_sem, zr_sem):
    n, m, count, block, length_x, pencil, rows = (
        dims["n"], dims["m"], dims["count"], dims["block"],
        dims["length_x"], dims["pencil"], dims["rows"])
    per = n - 1
    me = lax.axis_index("space")
    mq = lax.axis_index("dp")
    hops = sorted(range(1, n), key=lambda k: abs(k - n / 2))

    loads = [pltpu.make_async_copy(src, dst, in_sem.at[i]) for i, (src, dst) in enumerate(
        [(t1_hbm, t1_v), (x_hbm, x_v), (s_hbm, s_v), (w1_hbm, w1_v), (b_hbm, b_v),
         (w2_hbm, w2_v), (t2_hbm, t2_v)])]
    for load in loads:
        load.start()

    barrier = pltpu.get_barrier_semaphore()
    for k in range(1, n):
        pl.semaphore_signal(barrier, inc=1, device_id={"space": lax.rem(me + k, n)}, device_id_type=MESH)
    for k in range(1, m):
        pl.semaphore_signal(barrier, inc=1, device_id={"dp": lax.rem(mq + k, m)}, device_id_type=MESH)

    loads[0].wait()
    loads[1].wait()
    sends = []
    for b in range(count):
        lanes = slice(b * block, (b + 1) * block)
        psend[b] = dot(t1_v[...], x_v[:, lanes], 1, 0).astype(bf16).reshape(psend.shape[1:])
        if b == 0:
            pl.semaphore_wait(barrier, n - 1 + m - 1)
        for k in hops:
            peer = lax.rem(me + k, n)
            copy = pltpu.make_async_remote_copy(
                src_ref=psend.at[b, peer], dst_ref=precv.at[b, me],
                send_sem=ps_sem.at[b, k - 1], recv_sem=pr_sem.at[b, k - 1],
                device_id={"space": peer}, device_id_type=MESH)
            copy.start()
            sends.append(copy)
        precv[b, me] = psend[b, me]

    loads[2].wait()
    loads[3].wait()
    loads[4].wait()
    bias = b_v[...].astype(f32)
    total = length_x * pencil
    tile = math.gcd(total, 32)
    for b in range(count):
        lanes = slice(b * block, (b + 1) * block)
        w1 = stacked(w1_v[b, 0], w1_v[b, 1])
        pair = jnp.concatenate([s_v[0, :, lanes], s_v[1, :, lanes]], axis=1)
        z_v[...] = dot(pair, w1, 1, 0) + jnp.concatenate([bias[0:1, lanes], bias[1:2, lanes]], axis=1)

        def gelu(t, carry, b=b):
            at = pl.ds(pl.multiple_of(t * tile, tile), tile)
            z = z_v[at, :]
            cdf = 0.5 * (1.0 + lax.erf(z * inv_root_two))
            act[b, at, :] = (z * cdf).astype(bf16)
            slope[b, at, :] = cdf + z * jnp.exp(-0.5 * z * z) * inv_root_tau
            return carry

        lax.fori_loop(0, total // tile, gelu, 0)

    def fold_gradient(b):
        for k in range(1, m):
            drecv_copy(b, k).wait_recv()
        for s in range(n):
            value = gbuf[mq, b, s].astype(f32)
            for k in range(1, m):
                value = value + drecv[k - 1, b, s].astype(f32)
            zsend[b, s] = value.astype(gbuf.dtype)
        for k in hops:
            copy = zsend_copy(b, k)
            copy.start()
            sends.append(copy)

    def drecv_copy(b, k):
        peer = lax.rem(mq + k, m)
        return pltpu.make_async_remote_copy(
            src_ref=gbuf.at[peer, b], dst_ref=drecv.at[k - 1, b],
            send_sem=ds_sem.at[b, k - 1], recv_sem=dr_sem.at[b, k - 1],
            device_id={"dp": peer}, device_id_type=MESH)

    def zsend_copy(b, k):
        peer = lax.rem(me + k, n)
        return pltpu.make_async_remote_copy(
            src_ref=zsend.at[b, peer], dst_ref=zrecv.at[k - 1, b],
            send_sem=zs_sem.at[b, k - 1], recv_sem=zr_sem.at[b, k - 1],
            device_id={"space": peer}, device_id_type=MESH)

    piece = math.gcd(pencil, 16)
    loads[5].wait()
    qcopies = {}
    for b in range(count):
        lanes = slice(b * block, (b + 1) * block)
        for k in range(per):
            sends[b * per + k].wait_recv()
        for r in range(0, pencil, piece):
            planes = [(precv[b, x, r:r + piece, :].astype(f32),
                       precv[b, x, pencil + r:pencil + r + piece, :].astype(f32)) for x in range(length_x)]
            for kx, (re, im) in enumerate(transform(planes, -1.0)):
                at = slice(kx * pencil + r, kx * pencil + r + piece)
                gsc[at, 0:block] = (re * dims["forward_scale"]).astype(bf16)
                gsc[at, block:2 * block] = (im * dims["forward_scale"]).astype(bf16)
        grad = gsc[...]
        w1 = stacked(w1_v[b, 0], w1_v[b, 1])
        w2 = stacked(w2_v[b, 0], w2_v[b, 1])
        dz = (dot(grad, w2, 1, 1) * slope[b]).astype(bf16)
        dz_v[...] = dz
        ds_v[...] = dot(dz, w1, 1, 1)
        for r in range(0, pencil, piece):
            freqs = [(ds_v[kx * pencil + r:kx * pencil + r + piece, 0:block],
                      ds_v[kx * pencil + r:kx * pencil + r + piece, block:2 * block]) for kx in range(length_x)]
            for x, (re, im) in enumerate(transform(freqs, 1.0)):
                qsend[b, x, r:r + piece, :] = re.astype(bf16)
                qsend[b, x, pencil + r:pencil + r + piece, :] = im.astype(bf16)
        for k in hops:
            peer = lax.rem(me + k, n)
            copy = pltpu.make_async_remote_copy(
                src_ref=qsend.at[b, peer], dst_ref=qrecv.at[b, me],
                send_sem=qs_sem.at[b, k - 1], recv_sem=qr_sem.at[b, k - 1],
                device_id={"space": peer}, device_id_type=MESH)
            copy.start()
            qcopies[b, k] = copy
        qrecv[b, me] = qsend[b, me]

        pair = jnp.concatenate([s_v[0, :, lanes], s_v[1, :, lanes]], axis=1)
        for w, (left, right) in enumerate([(pair, dz_v[...]), (act[b], gsc[...])]):
            full = dot(left, right, 0, 0) * dims["grad_scale"]
            real = full[:block, :block] + full[block:, block:]
            imag = full[:block, block:] - full[block:, :block]
            for part, value in enumerate([real, imag]):
                for s in range(n):
                    for q in range(m):
                        at = (s * m + q) * rows
                        gbuf[q, b, s, w, part] = value[at:at + rows].astype(gbuf.dtype)
        for k in range(1, m):
            copy = drecv_copy(b, k)
            copy.start()
            sends.append(copy)
        if b > 0:
            fold_gradient(b - 1)

    fold_gradient(count - 1)
    outs = []
    loads[6].wait()
    for b in range(count):
        lanes = slice(b * block, (b + 1) * block)
        for k in range(1, n):
            qcopies[b, k].wait_recv()
        field = dot(t2_v[...], qrecv[b].reshape(t2_v.shape[1], block), 1, 0)
        gin_v[:, lanes] = (field * dims["inverse_scale"]).astype(bf16)
        copy = pltpu.make_async_copy(gin_v.at[:, lanes], gin_hbm.at[:, lanes], out_sem.at[b])
        copy.start()
        outs.append(copy)
    for b in range(count):
        for k in range(1, n):
            zsend_copy(b, k).wait_recv()
        value = zsend[b, me].astype(f32)
        for k in range(1, n):
            value = value + zrecv[k - 1, b].astype(f32)
        g1_v[b] = value[0]
        g2_v[b] = value[1]
    for i, (src, dst) in enumerate([(g1_v, g1_hbm), (g2_v, g2_hbm)]):
        copy = pltpu.make_async_copy(src, dst, out_sem.at[count + i])
        copy.start()
        outs.append(copy)
    for copy in sends:
        copy.wait_send()
    for copy in qcopies.values():
        copy.wait_send()
    for copy in outs:
        copy.wait()


def body(n, m, grad_out, saved_spectrum, w_first, bias_first, w_second):
    samples, planes, length_y, length_z, width = grad_out.shape
    count, _, block, _ = w_first.shape
    assert samples == 1 and planes == 1
    length_x = planes * n
    cells = length_x * length_y * length_z
    pencil = length_y // n * length_z
    area = length_y * length_z
    total = length_x * pencil
    rows = block // (n * m)
    factor, table = scaled_table(plane_table(length_y, length_z, n))
    norm = 1.0 / math.sqrt(cells)
    dims = dict(n=n, m=m, count=count, block=block, length_x=length_x, pencil=pencil, rows=rows,
                forward_scale=norm / factor, inverse_scale=norm / factor,
                grad_scale=1.0 / math.sqrt(cells * samples * m))
    kept = bf16 if rows % 16 == 0 else f32
    vmem = pltpu.VMEM
    dma = pltpu.SemaphoreType.DMA
    chunk = (2 * pencil, block)
    term = (2, 2, rows, block)
    any_spec = pl.BlockSpec(memory_space=pl.ANY)
    grad_in, grad_first, grad_second = pl.pallas_call(
        functools.partial(kernel, dims),
        out_shape=(
            jax.ShapeDtypeStruct((area, width), bf16),
            jax.ShapeDtypeStruct((count, 2, rows, block), f32),
            jax.ShapeDtypeStruct((count, 2, rows, block), f32),
        ),
        in_specs=[any_spec] * 7,
        out_specs=(any_spec,) * 3,
        scratch_shapes=[
            vmem((area, width), bf16), vmem((2, total, width), bf16), vmem(w_first.shape, bf16),
            vmem(bias_first.shape, bf16), vmem(w_second.shape, bf16),
            vmem(table.shape, bf16), vmem(table.shape[::-1], bf16),
            vmem((count, n) + chunk, bf16), vmem((count, n) + chunk, bf16),
            vmem((total, 2 * block), f32), vmem((count, total, 2 * block), bf16),
            vmem((count, total, 2 * block), f32), vmem((total, 2 * block), bf16),
            vmem((total, 2 * block), bf16), vmem((total, 2 * block), f32),
            vmem((count, n) + chunk, bf16), vmem((count, n) + chunk, bf16), vmem((area, width), bf16),
            vmem((m, count, n) + term, kept), vmem((max(m - 1, 1), count, n) + term, kept),
            vmem((count, n) + term, kept), vmem((max(n - 1, 1), count) + term, kept),
            vmem((count, 2, rows, block), f32), vmem((count, 2, rows, block), f32),
            dma((7,)), dma((count + 2,)),
            dma((count, n)), dma((count, n)), dma((count, n)), dma((count, n)),
            dma((count, m)), dma((count, m)), dma((count, n)), dma((count, n)),
        ],
        compiler_params=pltpu.CompilerParams(collective_id=0, has_side_effects=True),
        name="mixer",
    )(
        grad_out.reshape(area, width), saved_spectrum.reshape(2, total, width), w_first, bias_first, w_second,
        jnp.asarray(table), jnp.asarray(np.ascontiguousarray(table.T)),
    )
    return (grad_in.reshape(grad_out.shape), grad_first, grad_second)


def solution(mesh):
    in_specs = (
        P(("parts", "dp"), "space", None, None, "chan"),
        P(None, ("parts", "dp"), None, "space", None, "chan"),
        P("chan", None, None, None),
        P(None, "chan"),
        P("chan", None, None, None),
    )
    out_specs = (
        P(("parts", "dp"), "space", None, None, "chan"),
        P(("parts", "chan"), None, ("space", "dp"), None),
        P(("parts", "chan"), None, ("space", "dp"), None),
    )
    local = functools.partial(body, mesh.shape["space"], mesh.shape["dp"])
    return jax.shard_map(local, mesh=mesh, in_specs=in_specs, out_specs=out_specs, check_vma=False)
```

```python
import functools
import math

import jax
import jax.numpy as jnp
import ml_dtypes
import numpy as np
from jax import lax
from jax.experimental import pallas as pl
from jax.experimental.pallas import tpu as pltpu
from jax.sharding import PartitionSpec as P

inv_root_two = 1.0 / math.sqrt(2.0)
inv_root_tau = 1.0 / math.sqrt(2.0 * math.pi)
f32 = jnp.float32
bf16 = jnp.bfloat16
MESH = pl.DeviceIdType.MESH


def scaled_table(table):
    best = None
    for step in range(512):
        factor = 1.0 + step / 512.0
        exact = table * factor
        kept = exact.astype(ml_dtypes.bfloat16).astype(np.float64)
        fit = float((kept * table).sum() / (table * table).sum())
        error = float(((kept - fit * table) ** 2).sum() / (kept**2).sum())
        if best is None or error < best[0]:
            best = (error, fit, kept.astype(ml_dtypes.bfloat16))
    return best[1], best[2]


def plane_table(length_y, length_z, shards):
    ky = np.arange(length_y)[:, None, None, None]
    kz = np.arange(length_z)[None, :, None, None]
    y = np.arange(length_y)[None, None, :, None]
    z = np.arange(length_z)[None, None, None, :]
    angle = 2.0 * np.pi * (ky * y / length_y + kz * z / length_z)
    both = np.stack([np.cos(angle), -np.sin(angle)])
    both = np.round(both, 12)
    both = both.reshape(2, shards, length_y // shards, length_z, length_y * length_z)
    return both.transpose(1, 0, 2, 3, 4).reshape(2 * length_y * length_z, -1)


def times(value, factor):
    re, im = value
    c, s = factor.real, factor.imag
    if abs(s) < 1e-12:
        return (re, im) if abs(c - 1.0) < 1e-12 else (re * c, im * c)
    if abs(c) < 1e-12:
        if abs(s - 1.0) < 1e-12:
            return (-im, re)
        if abs(s + 1.0) < 1e-12:
            return (im, -re)
        return (-im * s, re * s)
    return (re * c - im * s, re * s + im * c)


def plus(a, b):
    return (a[0] + b[0], a[1] + b[1])


def minus(a, b):
    return (a[0] - b[0], a[1] - b[1])


def transform(values, orient):
    n = len(values)
    if n == 1:
        return values
    root = lambda k: complex(math.cos(2 * math.pi * k / n), orient * math.sin(2 * math.pi * k / n))
    if n % 2:
        out = []
        for k in range(n):
            total = values[0]
            for j in range(1, n):
                total = plus(total, times(values[j], root(k * j % n)))
            out.append(total)
        return out
    even = transform(values[0::2], orient)
    odd = transform(values[1::2], orient)
    turned = [times(odd[k], root(k)) for k in range(n // 2)]
    return [plus(even[k], turned[k]) for k in range(n // 2)] + [
        minus(even[k], turned[k]) for k in range(n // 2)
    ]


def reverse(index, bits):
    return sum(((index >> i) & 1) << (bits - 1 - i) for i in range(bits))


def dot(a, b, ca, cb):
    return lax.dot_general(a, b, (((ca,), (cb,)), ((), ())), preferred_element_type=f32)


def stacked(re, im):
    top = jnp.concatenate([re, im], axis=1)
    low = jnp.concatenate([-im, re], axis=1)
    return jnp.concatenate([top, low], axis=0)


def kernel(dims, x_hbm, s_hbm, w1_hbm, b_hbm, w2_hbm, t1_hbm, t2_hbm,
           gin_hbm, g1_hbm, g2_hbm,
           x_v, s_v, w1_v, b_v, w2_v, t1_v, t2_v,
           psend, precv, z_v, act, slope, gsc, dz_v, ds_v, qsend, qrecv, gin_v,
           gbuf, drecv, zbufs, zrecvs, g1_v, g2_v,
           in_sem, out_sem, ps_sem, pr_sem, qs_sem, qr_sem, ds_sem, dr_sem, zs_sem, zr_sem):
    n, m, count, block, length_x, pencil, rows = (
        dims["n"], dims["m"], dims["count"], dims["block"],
        dims["length_x"], dims["pencil"], dims["rows"])
    per = n - 1
    me = lax.axis_index("space")
    mq = lax.axis_index("dp")
    hops = sorted(range(1, n), key=lambda k: abs(k - n / 2))

    loads = [pltpu.make_async_copy(src, dst, in_sem.at[i]) for i, (src, dst) in enumerate(
        [(t1_hbm, t1_v), (x_hbm, x_v), (s_hbm, s_v), (w1_hbm, w1_v), (b_hbm, b_v),
         (w2_hbm, w2_v), (t2_hbm, t2_v)])]
    for load in loads:
        load.start()

    barrier = pltpu.get_barrier_semaphore()
    for k in range(1, n):
        pl.semaphore_signal(barrier, inc=1, device_id={"space": lax.rem(me + k, n)}, device_id_type=MESH)
    for k in range(1, m):
        pl.semaphore_signal(barrier, inc=1, device_id={"dp": lax.rem(mq + k, m)}, device_id_type=MESH)

    loads[0].wait()
    loads[1].wait()
    sends = []
    for b in range(count):
        lanes = slice(b * block, (b + 1) * block)
        psend[b] = dot(t1_v[...], x_v[:, lanes], 1, 0).astype(bf16).reshape(psend.shape[1:])
        if b == 0:
            pl.semaphore_wait(barrier, n - 1 + m - 1)
        for k in hops:
            peer = lax.rem(me + k, n)
            copy = pltpu.make_async_remote_copy(
                src_ref=psend.at[b, peer], dst_ref=precv.at[b, me],
                send_sem=ps_sem.at[b, k - 1], recv_sem=pr_sem.at[b, k - 1],
                device_id={"space": peer}, device_id_type=MESH)
            copy.start()
            sends.append(copy)
        precv[b, me] = psend[b, me]

    loads[2].wait()
    loads[3].wait()
    loads[4].wait()
    bias = b_v[...].astype(f32)
    total = length_x * pencil
    tile = math.gcd(total, 32)
    for b in range(count):
        lanes = slice(b * block, (b + 1) * block)
        w1 = stacked(w1_v[b, 0], w1_v[b, 1])
        pair = jnp.concatenate([s_v[0, :, lanes], s_v[1, :, lanes]], axis=1)
        z_v[...] = dot(pair, w1, 1, 0) + jnp.concatenate([bias[0:1, lanes], bias[1:2, lanes]], axis=1)

        def gelu(t, carry, b=b):
            at = pl.ds(pl.multiple_of(t * tile, tile), tile)
            z = z_v[at, :]
            cdf = 0.5 * (1.0 + lax.erf(z * inv_root_two))
            act[b, at, :] = (z * cdf).astype(bf16)
            slope[b, at, :] = cdf + z * jnp.exp(-0.5 * z * z) * inv_root_tau
            return carry

        lax.fori_loop(0, total // tile, gelu, 0)

    levels = len(zbufs) - 1

    def drecv_copy(b, k):
        peer = lax.rem(mq + k, m)
        return pltpu.make_async_remote_copy(
            src_ref=gbuf.at[peer, b], dst_ref=drecv.at[k - 1, b],
            send_sem=ds_sem.at[b, k - 1], recv_sem=dr_sem.at[b, k - 1],
            device_id={"dp": peer}, device_id_type=MESH)

    def level_copy(b, j):
        half = n >> (j + 1)
        bit = lax.rem(me // (1 << j), 2)
        return pltpu.make_async_remote_copy(
            src_ref=zbufs[j].at[b, pl.ds((1 - bit) * half, half)], dst_ref=zrecvs[j].at[b],
            send_sem=zs_sem.at[b, j], recv_sem=zr_sem.at[b, j],
            device_id={"space": me + (1 - 2 * bit) * (1 << j)}, device_id_type=MESH)

    def fold_gradient(b, j):
        if j == 0:
            for k in range(1, m):
                drecv_copy(b, k).wait_recv()
            for s in range(n):
                value = gbuf[mq, b, s].astype(f32)
                for k in range(1, m):
                    value = value + drecv[k - 1, b, s].astype(f32)
                zbufs[0][b, s] = value.astype(zbufs[0].dtype)
        else:
            level_copy(b, j - 1).wait_recv()
            half = n >> j
            bit = lax.rem(me // (1 << (j - 1)), 2)
            for s in range(half):
                value = zbufs[j - 1][b, bit * half + s].astype(f32) + zrecvs[j - 1][b, s].astype(f32)
                zbufs[j][b, s] = value.astype(zbufs[j].dtype)
        if j < levels:
            copy = level_copy(b, j)
            copy.start()
            sends.append(copy)

    piece = math.gcd(pencil, 16)
    loads[5].wait()
    qcopies = {}
    for b in range(count):
        lanes = slice(b * block, (b + 1) * block)
        for k in range(per):
            sends[b * per + k].wait_recv()
        for r in range(0, pencil, piece):
            planes = [(precv[b, x, r:r + piece, :].astype(f32),
                       precv[b, x, pencil + r:pencil + r + piece, :].astype(f32)) for x in range(length_x)]
            for kx, (re, im) in enumerate(transform(planes, -1.0)):
                at = slice(kx * pencil + r, kx * pencil + r + piece)
                gsc[at, 0:block] = (re * dims["forward_scale"]).astype(bf16)
                gsc[at, block:2 * block] = (im * dims["forward_scale"]).astype(bf16)
        grad = gsc[...]
        w1 = stacked(w1_v[b, 0], w1_v[b, 1])
        w2 = stacked(w2_v[b, 0], w2_v[b, 1])
        dz = (dot(grad, w2, 1, 1) * slope[b]).astype(bf16)
        dz_v[...] = dz
        ds_v[...] = dot(dz, w1, 1, 1)
        for r in range(0, pencil, piece):
            freqs = [(ds_v[kx * pencil + r:kx * pencil + r + piece, 0:block],
                      ds_v[kx * pencil + r:kx * pencil + r + piece, block:2 * block]) for kx in range(length_x)]
            for x, (re, im) in enumerate(transform(freqs, 1.0)):
                qsend[b, x, r:r + piece, :] = re.astype(bf16)
                qsend[b, x, pencil + r:pencil + r + piece, :] = im.astype(bf16)
        for k in hops:
            peer = lax.rem(me + k, n)
            copy = pltpu.make_async_remote_copy(
                src_ref=qsend.at[b, peer], dst_ref=qrecv.at[b, me],
                send_sem=qs_sem.at[b, k - 1], recv_sem=qr_sem.at[b, k - 1],
                device_id={"space": peer}, device_id_type=MESH)
            copy.start()
            qcopies[b, k] = copy
        qrecv[b, me] = qsend[b, me]

        pair = jnp.concatenate([s_v[0, :, lanes], s_v[1, :, lanes]], axis=1)
        for w, (left, right) in enumerate([(pair, dz_v[...]), (act[b], gsc[...])]):
            full = dot(left, right, 0, 0) * dims["grad_scale"]
            real = full[:block, :block] + full[block:, block:]
            imag = full[:block, block:] - full[block:, :block]
            for part, value in enumerate([real, imag]):
                for s in range(n):
                    for q in range(m):
                        at = (s * m + q) * rows
                        gbuf[q, b, reverse(s, levels), w, part] = value[at:at + rows].astype(gbuf.dtype)
        for k in range(1, m):
            copy = drecv_copy(b, k)
            copy.start()
            sends.append(copy)
        for j in range(min(b, levels)):
            fold_gradient(b - 1 - j, j)

    for b in range(count, count + levels + 1):
        for j in range(levels + 1):
            if 0 <= b - 1 - j < count and j < levels:
                fold_gradient(b - 1 - j, j)
    outs = []
    loads[6].wait()
    for b in range(count):
        lanes = slice(b * block, (b + 1) * block)
        for k in range(1, n):
            qcopies[b, k].wait_recv()
        field = dot(t2_v[...], qrecv[b].reshape(t2_v.shape[1], block), 1, 0)
        gin_v[:, lanes] = (field * dims["inverse_scale"]).astype(bf16)
        copy = pltpu.make_async_copy(gin_v.at[:, lanes], gin_hbm.at[:, lanes], out_sem.at[b])
        copy.start()
        outs.append(copy)
    for b in range(count):
        fold_gradient(b, levels)
        g1_v[b] = zbufs[levels][b, 0, 0].astype(f32)
        g2_v[b] = zbufs[levels][b, 0, 1].astype(f32)
    for i, (src, dst) in enumerate([(g1_v, g1_hbm), (g2_v, g2_hbm)]):
        copy = pltpu.make_async_copy(src, dst, out_sem.at[count + i])
        copy.start()
        outs.append(copy)
    for copy in sends:
        copy.wait_send()
    for copy in qcopies.values():
        copy.wait_send()
    for copy in outs:
        copy.wait()


def body(n, m, grad_out, saved_spectrum, w_first, bias_first, w_second):
    samples, planes, length_y, length_z, width = grad_out.shape
    count, _, block, _ = w_first.shape
    assert samples == 1 and planes == 1
    length_x = planes * n
    cells = length_x * length_y * length_z
    pencil = length_y // n * length_z
    area = length_y * length_z
    total = length_x * pencil
    rows = block // (n * m)
    factor, table = scaled_table(plane_table(length_y, length_z, n))
    norm = 1.0 / math.sqrt(cells)
    dims = dict(n=n, m=m, count=count, block=block, length_x=length_x, pencil=pencil, rows=rows,
                forward_scale=norm / factor, inverse_scale=norm / factor,
                grad_scale=1.0 / math.sqrt(cells * samples * m))
    levels = n.bit_length() - 1
    assert n == 1 << levels
    kept = bf16 if rows % 16 == 0 else f32
    vmem = pltpu.VMEM
    dma = pltpu.SemaphoreType.DMA
    chunk = (2 * pencil, block)
    term = (2, 2, rows, block)
    any_spec = pl.BlockSpec(memory_space=pl.ANY)
    grad_in, grad_first, grad_second = pl.pallas_call(
        functools.partial(kernel, dims),
        out_shape=(
            jax.ShapeDtypeStruct((area, width), bf16),
            jax.ShapeDtypeStruct((count, 2, rows, block), f32),
            jax.ShapeDtypeStruct((count, 2, rows, block), f32),
        ),
        in_specs=[any_spec] * 7,
        out_specs=(any_spec,) * 3,
        scratch_shapes=[
            vmem((area, width), bf16), vmem((2, total, width), bf16), vmem(w_first.shape, bf16),
            vmem(bias_first.shape, bf16), vmem(w_second.shape, bf16),
            vmem(table.shape, bf16), vmem(table.shape[::-1], bf16),
            vmem((count, n) + chunk, bf16), vmem((count, n) + chunk, bf16),
            vmem((total, 2 * block), f32), vmem((count, total, 2 * block), bf16),
            vmem((count, total, 2 * block), f32), vmem((total, 2 * block), bf16),
            vmem((total, 2 * block), bf16), vmem((total, 2 * block), f32),
            vmem((count, n) + chunk, bf16), vmem((count, n) + chunk, bf16), vmem((area, width), bf16),
            vmem((m, count, n) + term, kept), vmem((max(m - 1, 1), count, n) + term, kept),
            tuple(vmem((count, n >> j) + term, kept if j < levels else f32) for j in range(levels + 1)),
            tuple(vmem((count, max(n >> (j + 1), 1)) + term, kept) for j in range(levels)),
            vmem((count, 2, rows, block), f32), vmem((count, 2, rows, block), f32),
            dma((7,)), dma((count + 2,)),
            dma((count, n)), dma((count, n)), dma((count, n)), dma((count, n)),
            dma((count, m)), dma((count, m)), dma((count, n)), dma((count, n)),
        ],
        compiler_params=pltpu.CompilerParams(collective_id=0, has_side_effects=True),
        name="mixer",
    )(
        grad_out.reshape(area, width), saved_spectrum.reshape(2, total, width), w_first, bias_first, w_second,
        jnp.asarray(table), jnp.asarray(np.ascontiguousarray(table.T)),
    )
    return (grad_in.reshape(grad_out.shape), grad_first, grad_second)


def solution(mesh):
    in_specs = (
        P(("parts", "dp"), "space", None, None, "chan"),
        P(None, ("parts", "dp"), None, "space", None, "chan"),
        P("chan", None, None, None),
        P(None, "chan"),
        P("chan", None, None, None),
    )
    out_specs = (
        P(("parts", "dp"), "space", None, None, "chan"),
        P(("parts", "chan"), None, ("space", "dp"), None),
        P(("parts", "chan"), None, ("space", "dp"), None),
    )
    local = functools.partial(body, mesh.shape["space"], mesh.shape["dp"])
    return jax.shard_map(local, mesh=mesh, in_specs=in_specs, out_specs=out_specs, check_vma=False)
```

```python
import functools
import math

import jax
import jax.numpy as jnp
import ml_dtypes
import numpy as np
from jax import lax
from jax.experimental import pallas as pl
from jax.experimental.pallas import tpu as pltpu
from jax.sharding import PartitionSpec as P

inv_root_two = 1.0 / math.sqrt(2.0)
inv_root_tau = 1.0 / math.sqrt(2.0 * math.pi)
f32 = jnp.float32
bf16 = jnp.bfloat16
MESH = pl.DeviceIdType.MESH


def scaled_table(table):
    best = None
    for step in range(512):
        factor = 1.0 + step / 512.0
        exact = table * factor
        kept = exact.astype(ml_dtypes.bfloat16).astype(np.float64)
        fit = float((kept * table).sum() / (table * table).sum())
        error = float(((kept - fit * table) ** 2).sum() / (kept**2).sum())
        if best is None or error < best[0]:
            best = (error, fit, kept.astype(ml_dtypes.bfloat16))
    return best[1], best[2]


def plane_table(length_y, length_z, shards):
    ky = np.arange(length_y)[:, None, None, None]
    kz = np.arange(length_z)[None, :, None, None]
    y = np.arange(length_y)[None, None, :, None]
    z = np.arange(length_z)[None, None, None, :]
    angle = 2.0 * np.pi * (ky * y / length_y + kz * z / length_z)
    both = np.stack([np.cos(angle), -np.sin(angle)])
    both = np.round(both, 12)
    local = length_y // shards
    both = both.reshape(2, shards, local, length_z, length_y * length_z).transpose(1, 0, 2, 3, 4)
    half = length_z // 2
    chunks = []
    for d in range(shards):
        first = both[d, :, 0].reshape(2 * length_z, -1)
        if d % (shards // 2) == 0:
            first = np.concatenate([first[: half + 1], first[length_z + 1 : length_z + half], 0 * first[:length_z]])
        chunks += [both[d, :, 1:].reshape(2 * (local - 1) * length_z, first.shape[1]), first]
    return np.concatenate(chunks)


def mirror_table(length_z):
    half = length_z // 2
    out = np.zeros((2 * length_z, length_z))
    for k in range(length_z):
        out[k, min(k, length_z - k)] = 1.0
        if k % half:
            out[length_z + k, half + min(k, length_z - k)] = 1.0 if k < half else -1.0
    return out


def times(value, factor):
    re, im = value
    c, s = factor.real, factor.imag
    if abs(s) < 1e-12:
        return (re, im) if abs(c - 1.0) < 1e-12 else (re * c, im * c)
    if abs(c) < 1e-12:
        if abs(s - 1.0) < 1e-12:
            return (-im, re)
        if abs(s + 1.0) < 1e-12:
            return (im, -re)
        return (-im * s, re * s)
    return (re * c - im * s, re * s + im * c)


def plus(a, b):
    return (a[0] + b[0], a[1] + b[1])


def minus(a, b):
    return (a[0] - b[0], a[1] - b[1])


def transform(values, orient):
    n = len(values)
    if n == 1:
        return values
    root = lambda k: complex(math.cos(2 * math.pi * k / n), orient * math.sin(2 * math.pi * k / n))
    if n % 2:
        out = []
        for k in range(n):
            total = values[0]
            for j in range(1, n):
                total = plus(total, times(values[j], root(k * j % n)))
            out.append(total)
        return out
    even = transform(values[0::2], orient)
    odd = transform(values[1::2], orient)
    turned = [times(odd[k], root(k)) for k in range(n // 2)]
    return [plus(even[k], turned[k]) for k in range(n // 2)] + [
        minus(even[k], turned[k]) for k in range(n // 2)
    ]


def reverse(index, bits):
    return sum(((index >> i) & 1) << (bits - 1 - i) for i in range(bits))


def dot(a, b, ca, cb):
    return lax.dot_general(a, b, (((ca,), (cb,)), ((), ())), preferred_element_type=f32)


def stacked(re, im):
    top = jnp.concatenate([re, im], axis=1)
    low = jnp.concatenate([-im, re], axis=1)
    return jnp.concatenate([top, low], axis=0)


def kernel(dims, x_hbm, s_hbm, w1_hbm, b_hbm, w2_hbm, t1_hbm, t2_hbm, mt_hbm,
           gin_hbm, g1_hbm, g2_hbm,
           x_v, s_v, w1_v, b_v, w2_v, t1_v, t2_v, mt_v,
           psend, precv, z_v, act, slope, gsc, dz_v, ds_v, qsend, qrecv, gin_v,
           gbuf, drecv, zbufs, zrecvs, g1_v, g2_v,
           in_sem, out_sem, ps_sem, pr_sem, qs_sem, qr_sem, ds_sem, dr_sem, zs_sem, zr_sem):
    n, m, count, block, length_x, pencil, rows = (
        dims["n"], dims["m"], dims["count"], dims["block"],
        dims["length_x"], dims["pencil"], dims["rows"])
    me = lax.axis_index("space")
    mq = lax.axis_index("dp")
    hops = sorted(range(1, n), key=lambda k: abs(k - n / 2))

    line = dims["line"]
    full = 2 * pencil
    short = full - line
    head = full - 2 * line

    def special(shard):
        return lax.rem(shard, n // 2) == 0

    def exchange(send, recv, send_sems, recv_sems, b, k, size):
        peer = lax.rem(me + k, n)
        return pltpu.make_async_remote_copy(
            src_ref=send.at[b, peer, 0:size], dst_ref=recv.at[b, me, 0:size],
            send_sem=send_sems.at[b, k - 1], recv_sem=recv_sems.at[b, k - 1],
            device_id={"space": peer}, device_id_type=MESH)

    def guarded(mirrored, act_on):
        @pl.when(mirrored)
        def _():
            act_on(short)

        @pl.when(jnp.logical_not(mirrored))
        def _():
            act_on(full)

    def first_exchange(b, k, size):
        return exchange(psend, precv, ps_sem, pr_sem, b, k, size)

    def second_exchange(b, k, size):
        return exchange(qsend, qrecv, qs_sem, qr_sem, b, k, size)

    loads = [pltpu.make_async_copy(src, dst, in_sem.at[i]) for i, (src, dst) in enumerate(
        [(t1_hbm, t1_v), (x_hbm, x_v), (s_hbm, s_v), (w1_hbm, w1_v), (b_hbm, b_v),
         (w2_hbm, w2_v), (t2_hbm, t2_v), (mt_hbm, mt_v)])]
    for load in loads:
        load.start()

    barrier = pltpu.get_barrier_semaphore()
    for k in range(1, n):
        pl.semaphore_signal(barrier, inc=1, device_id={"space": lax.rem(me + k, n)}, device_id_type=MESH)
    for k in range(1, m):
        pl.semaphore_signal(barrier, inc=1, device_id={"dp": lax.rem(mq + k, m)}, device_id_type=MESH)

    for b in range(count):
        for d in range(0, n, n // 2):
            qrecv[b, d, short:full, :] = jnp.zeros((line, block), bf16)
    loads[0].wait()
    loads[1].wait()
    sends = []
    for b in range(count):
        lanes = slice(b * block, (b + 1) * block)
        psend[b] = dot(t1_v[...], x_v[:, lanes], 1, 0).astype(bf16).reshape(psend.shape[1:])
        if b == 0:
            pl.semaphore_wait(barrier, n - 1 + m - 1)
        for k in hops:
            guarded(special(lax.rem(me + k, n)), lambda size: first_exchange(b, k, size).start())
        precv[b, me] = psend[b, me]

    loads[2].wait()
    loads[3].wait()
    loads[4].wait()
    bias = b_v[...].astype(f32)
    total = length_x * pencil
    tile = math.gcd(total, 32)
    for b in range(count):
        lanes = slice(b * block, (b + 1) * block)
        w1 = stacked(w1_v[b, 0], w1_v[b, 1])
        pair = jnp.concatenate([s_v[0, :, lanes], s_v[1, :, lanes]], axis=1)
        z_v[...] = dot(pair, w1, 1, 0) + jnp.concatenate([bias[0:1, lanes], bias[1:2, lanes]], axis=1)

        def gelu(t, carry, b=b):
            at = pl.ds(pl.multiple_of(t * tile, tile), tile)
            z = z_v[at, :]
            cdf = 0.5 * (1.0 + lax.erf(z * inv_root_two))
            act[b, at, :] = (z * cdf).astype(bf16)
            slope[b, at, :] = cdf + z * jnp.exp(-0.5 * z * z) * inv_root_tau
            return carry

        lax.fori_loop(0, total // tile, gelu, 0)

    levels = len(zbufs) - 1

    def drecv_copy(b, k):
        peer = lax.rem(mq + k, m)
        return pltpu.make_async_remote_copy(
            src_ref=gbuf.at[peer, b], dst_ref=drecv.at[k - 1, b],
            send_sem=ds_sem.at[b, k - 1], recv_sem=dr_sem.at[b, k - 1],
            device_id={"dp": peer}, device_id_type=MESH)

    def level_copy(b, j):
        half = n >> (j + 1)
        bit = lax.rem(me // (1 << j), 2)
        return pltpu.make_async_remote_copy(
            src_ref=zbufs[j].at[b, pl.ds((1 - bit) * half, half)], dst_ref=zrecvs[j].at[b],
            send_sem=zs_sem.at[b, j], recv_sem=zr_sem.at[b, j],
            device_id={"space": me + (1 - 2 * bit) * (1 << j)}, device_id_type=MESH)

    def fold_gradient(b, j):
        if j == 0:
            for k in range(1, m):
                drecv_copy(b, k).wait_recv()
            for s in range(n):
                value = gbuf[mq, b, s].astype(f32)
                for k in range(1, m):
                    value = value + drecv[k - 1, b, s].astype(f32)
                zbufs[0][b, s] = value.astype(zbufs[0].dtype)
        else:
            level_copy(b, j - 1).wait_recv()
            half = n >> j
            bit = lax.rem(me // (1 << (j - 1)), 2)
            for s in range(half):
                value = zbufs[j - 1][b, bit * half + s].astype(f32) + zrecvs[j - 1][b, s].astype(f32)
                zbufs[j][b, s] = value.astype(zbufs[j].dtype)
        if j < levels:
            copy = level_copy(b, j)
            copy.start()
            sends.append(copy)

    places = [(head, short)] + [
        (k * line, head // 2 + k * line) for k in range(pencil // line - 1)]
    loads[5].wait()
    loads[7].wait()
    for b in range(count):
        lanes = slice(b * block, (b + 1) * block)
        for k in range(1, n):
            guarded(special(me), lambda size: first_exchange(b, k, size).wait_recv())

        @pl.when(special(me))
        def _():
            for x in range(length_x):
                spread = dot(mt_v[...], precv[b, x, head:short, :], 1, 0)
                precv[b, x, head:full, :] = spread.astype(bf16)

        for r in range(0, pencil, line):
            re_at, im_at = places[r // line]
            planes = [(precv[b, x, re_at:re_at + line, :].astype(f32),
                       precv[b, x, im_at:im_at + line, :].astype(f32)) for x in range(length_x)]
            for kx, (re, im) in enumerate(transform(planes, -1.0)):
                at = slice(kx * pencil + r, kx * pencil + r + line)
                gsc[at, 0:block] = (re * dims["forward_scale"]).astype(bf16)
                gsc[at, block:2 * block] = (im * dims["forward_scale"]).astype(bf16)
        grad = gsc[...]
        w1 = stacked(w1_v[b, 0], w1_v[b, 1])
        w2 = stacked(w2_v[b, 0], w2_v[b, 1])
        dz = (dot(grad, w2, 1, 1) * slope[b]).astype(bf16)
        dz_v[...] = dz
        ds_v[...] = dot(dz, w1, 1, 1)
        for r in range(0, pencil, line):
            re_at, im_at = places[r // line]
            freqs = [(ds_v[kx * pencil + r:kx * pencil + r + line, 0:block],
                      ds_v[kx * pencil + r:kx * pencil + r + line, block:2 * block]) for kx in range(length_x)]
            for x, (re, im) in enumerate(transform(freqs, 1.0)):
                qsend[b, x, re_at:re_at + line, :] = re.astype(bf16)
                qsend[b, x, im_at:im_at + line, :] = im.astype(bf16)

        @pl.when(special(me))
        def _():
            for x in range(length_x):
                merged = dot(mt_v[...], qsend[b, x, head:full, :], 0, 0)
                qsend[b, x, head:short, :] = merged.astype(bf16)

        for k in hops:
            guarded(special(me), lambda size: second_exchange(b, k, size).start())
        qrecv[b, me] = qsend[b, me]

        pair = jnp.concatenate([s_v[0, :, lanes], s_v[1, :, lanes]], axis=1)
        for w, (left, right) in enumerate([(pair, dz_v[...]), (act[b], gsc[...])]):
            outer = dot(left, right, 0, 0) * dims["grad_scale"]
            real = outer[:block, :block] + outer[block:, block:]
            imag = outer[:block, block:] - outer[block:, :block]
            for part, value in enumerate([real, imag]):
                for s in range(n):
                    for q in range(m):
                        at = (s * m + q) * rows
                        gbuf[q, b, reverse(s, levels), w, part] = value[at:at + rows].astype(gbuf.dtype)
        for k in range(1, m):
            copy = drecv_copy(b, k)
            copy.start()
            sends.append(copy)
        for j in range(min(b, levels)):
            fold_gradient(b - 1 - j, j)

    for b in range(count, count + levels + 1):
        for j in range(levels + 1):
            if 0 <= b - 1 - j < count and j < levels:
                fold_gradient(b - 1 - j, j)
    outs = []
    loads[6].wait()
    for b in range(count):
        lanes = slice(b * block, (b + 1) * block)
        for k in range(1, n):
            guarded(special(lax.rem(me + n - k, n)), lambda size: second_exchange(b, k, size).wait_recv())
        field = dot(t2_v[...], qrecv[b].reshape(t2_v.shape[1], block), 1, 0)
        gin_v[:, lanes] = (field * dims["inverse_scale"]).astype(bf16)
        copy = pltpu.make_async_copy(gin_v.at[:, lanes], gin_hbm.at[:, lanes], out_sem.at[b])
        copy.start()
        outs.append(copy)
    for b in range(count):
        fold_gradient(b, levels)
        g1_v[b] = zbufs[levels][b, 0, 0].astype(f32)
        g2_v[b] = zbufs[levels][b, 0, 1].astype(f32)
    for i, (src, dst) in enumerate([(g1_v, g1_hbm), (g2_v, g2_hbm)]):
        copy = pltpu.make_async_copy(src, dst, out_sem.at[count + i])
        copy.start()
        outs.append(copy)
    for copy in sends:
        copy.wait_send()
    for b in range(count):
        for k in range(1, n):
            guarded(special(lax.rem(me + k, n)), lambda size: first_exchange(b, k, size).wait_send())
            guarded(special(me), lambda size: second_exchange(b, k, size).wait_send())
    for copy in outs:
        copy.wait()


def body(n, m, grad_out, saved_spectrum, w_first, bias_first, w_second):
    samples, planes, length_y, length_z, width = grad_out.shape
    count, _, block, _ = w_first.shape
    assert samples == 1 and planes == 1
    length_x = planes * n
    cells = length_x * length_y * length_z
    pencil = length_y // n * length_z
    area = length_y * length_z
    total = length_x * pencil
    rows = block // (n * m)
    factor, table = scaled_table(plane_table(length_y, length_z, n))
    norm = 1.0 / math.sqrt(cells)
    dims = dict(n=n, m=m, count=count, block=block, length_x=length_x, pencil=pencil, rows=rows, line=length_z,
                forward_scale=norm / factor, inverse_scale=norm / factor,
                grad_scale=1.0 / math.sqrt(cells * samples * m))
    levels = n.bit_length() - 1
    assert n == 1 << levels
    kept = bf16 if rows % 16 == 0 else f32
    vmem = pltpu.VMEM
    dma = pltpu.SemaphoreType.DMA
    chunk = (2 * pencil, block)
    term = (2, 2, rows, block)
    any_spec = pl.BlockSpec(memory_space=pl.ANY)
    grad_in, grad_first, grad_second = pl.pallas_call(
        functools.partial(kernel, dims),
        out_shape=(
            jax.ShapeDtypeStruct((area, width), bf16),
            jax.ShapeDtypeStruct((count, 2, rows, block), f32),
            jax.ShapeDtypeStruct((count, 2, rows, block), f32),
        ),
        in_specs=[any_spec] * 8,
        out_specs=(any_spec,) * 3,
        scratch_shapes=[
            vmem((area, width), bf16), vmem((2, total, width), bf16), vmem(w_first.shape, bf16),
            vmem(bias_first.shape, bf16), vmem(w_second.shape, bf16),
            vmem(table.shape, bf16), vmem(table.shape[::-1], bf16), vmem((2 * length_z, length_z), bf16),
            vmem((count, n) + chunk, bf16), vmem((count, n) + chunk, bf16),
            vmem((total, 2 * block), f32), vmem((count, total, 2 * block), bf16),
            vmem((count, total, 2 * block), f32), vmem((total, 2 * block), bf16),
            vmem((total, 2 * block), bf16), vmem((total, 2 * block), f32),
            vmem((count, n) + chunk, bf16), vmem((count, n) + chunk, bf16), vmem((area, width), bf16),
            vmem((m, count, n) + term, kept), vmem((max(m - 1, 1), count, n) + term, kept),
            tuple(vmem((count, n >> j) + term, kept if j < levels else f32) for j in range(levels + 1)),
            tuple(vmem((count, max(n >> (j + 1), 1)) + term, kept) for j in range(levels)),
            vmem((count, 2, rows, block), f32), vmem((count, 2, rows, block), f32),
            dma((8,)), dma((count + 2,)),
            dma((count, n)), dma((count, n)), dma((count, n)), dma((count, n)),
            dma((count, m)), dma((count, m)), dma((count, n)), dma((count, n)),
        ],
        compiler_params=pltpu.CompilerParams(collective_id=0, has_side_effects=True),
        name="mixer",
    )(
        grad_out.reshape(area, width), saved_spectrum.reshape(2, total, width), w_first, bias_first, w_second,
        jnp.asarray(table), jnp.asarray(np.ascontiguousarray(table.T)),
        jnp.asarray(mirror_table(length_z).astype(ml_dtypes.bfloat16)),
    )
    def place(a, b, c, d, e, f, a_v, b_v, c_v, in_sem, out_sem):
        quarter = area // 4
        moves = [(b, b_v, e), (c, c_v, f)] + [
            (a.at[i * quarter:(i + 1) * quarter], a_v.at[i * quarter:(i + 1) * quarter], d.at[i * quarter:(i + 1) * quarter])
            for i in range(4)]
        loads = [pltpu.make_async_copy(x, y, in_sem.at[i]) for i, (x, y, _) in enumerate(moves)]
        stores = [pltpu.make_async_copy(y, z, out_sem.at[i]) for i, (_, y, z) in enumerate(moves)]
        for load in loads:
            load.start()
        for load, store in zip(loads, stores):
            load.wait()
            store.start()
        for store in stores:
            store.wait()

    grad_in, grad_first, grad_second = pl.pallas_call(
        place,
        out_shape=tuple(jax.ShapeDtypeStruct(a.shape, a.dtype) for a in (grad_in, grad_first, grad_second)),
        in_specs=[any_spec] * 3, out_specs=(any_spec,) * 3,
        scratch_shapes=[vmem(a.shape, a.dtype) for a in (grad_in, grad_first, grad_second)] + [dma((6,)), dma((6,))],
        name="place",
    )(grad_in, grad_first, grad_second)
    return (grad_in.reshape(grad_out.shape), grad_first, grad_second)


def solution(mesh):
    in_specs = (
        P(("parts", "dp"), "space", None, None, "chan"),
        P(None, ("parts", "dp"), None, "space", None, "chan"),
        P("chan", None, None, None),
        P(None, "chan"),
        P("chan", None, None, None),
    )
    out_specs = (
        P(("parts", "dp"), "space", None, None, "chan"),
        P(("parts", "chan"), None, ("space", "dp"), None),
        P(("parts", "chan"), None, ("space", "dp"), None),
    )
    local = functools.partial(body, mesh.shape["space"], mesh.shape["dp"])
    return jax.shard_map(local, mesh=mesh, in_specs=in_specs, out_specs=out_specs, check_vma=False)
```

```python
import functools
import math

import jax
import jax.numpy as jnp
import ml_dtypes
import numpy as np
from jax import lax
from jax.experimental import pallas as pl
from jax.experimental.pallas import tpu as pltpu
from jax.sharding import PartitionSpec as P

inv_root_two = 1.0 / math.sqrt(2.0)
inv_root_tau = 1.0 / math.sqrt(2.0 * math.pi)
f32 = jnp.float32
bf16 = jnp.bfloat16
MESH = pl.DeviceIdType.MESH


def scaled_table(table):
    best = None
    for step in range(512):
        factor = 1.0 + step / 512.0
        exact = table * factor
        kept = exact.astype(ml_dtypes.bfloat16).astype(np.float64)
        fit = float((kept * table).sum() / (table * table).sum())
        error = float(((kept - fit * table) ** 2).sum() / (kept**2).sum())
        if best is None or error < best[0]:
            best = (error, fit, kept.astype(ml_dtypes.bfloat16))
    return best[1], best[2]


def plane_table(length_y, length_z, shards):
    ky = np.arange(length_y)[:, None, None, None]
    kz = np.arange(length_z)[None, :, None, None]
    y = np.arange(length_y)[None, None, :, None]
    z = np.arange(length_z)[None, None, None, :]
    angle = 2.0 * np.pi * (ky * y / length_y + kz * z / length_z)
    both = np.stack([np.cos(angle), -np.sin(angle)])
    both = np.round(both, 12)
    local = length_y // shards
    both = both.reshape(2, shards, local, length_z, length_y * length_z).transpose(1, 0, 2, 3, 4)
    half = length_z // 2
    chunks = []
    for d in range(shards):
        first = both[d, :, 0].reshape(2 * length_z, -1)
        if d % (shards // 2) == 0:
            first = np.concatenate([first[: half + 1], first[length_z + 1 : length_z + half], 0 * first[:length_z]])
        chunks += [both[d, :, 1:].reshape(2 * (local - 1) * length_z, first.shape[1]), first]
    return np.concatenate(chunks)


def mirror_table(length_z):
    half = length_z // 2
    out = np.zeros((2 * length_z, length_z))
    for k in range(length_z):
        out[k, min(k, length_z - k)] = 1.0
        if k % half:
            out[length_z + k, half + min(k, length_z - k)] = 1.0 if k < half else -1.0
    return out


def times(value, factor):
    re, im = value
    c, s = factor.real, factor.imag
    if abs(s) < 1e-12:
        return (re, im) if abs(c - 1.0) < 1e-12 else (re * c, im * c)
    if abs(c) < 1e-12:
        if abs(s - 1.0) < 1e-12:
            return (-im, re)
        if abs(s + 1.0) < 1e-12:
            return (im, -re)
        return (-im * s, re * s)
    return (re * c - im * s, re * s + im * c)


def plus(a, b):
    return (a[0] + b[0], a[1] + b[1])


def minus(a, b):
    return (a[0] - b[0], a[1] - b[1])


def transform(values, orient):
    n = len(values)
    if n == 1:
        return values
    root = lambda k: complex(math.cos(2 * math.pi * k / n), orient * math.sin(2 * math.pi * k / n))
    if n % 2:
        out = []
        for k in range(n):
            total = values[0]
            for j in range(1, n):
                total = plus(total, times(values[j], root(k * j % n)))
            out.append(total)
        return out
    even = transform(values[0::2], orient)
    odd = transform(values[1::2], orient)
    turned = [times(odd[k], root(k)) for k in range(n // 2)]
    return [plus(even[k], turned[k]) for k in range(n // 2)] + [
        minus(even[k], turned[k]) for k in range(n // 2)
    ]


def reverse(index, bits):
    return sum(((index >> i) & 1) << (bits - 1 - i) for i in range(bits))


def dot(a, b, ca, cb):
    return lax.dot_general(a, b, (((ca,), (cb,)), ((), ())), preferred_element_type=f32)


def stacked(re, im):
    top = jnp.concatenate([re, im], axis=1)
    low = jnp.concatenate([-im, re], axis=1)
    return jnp.concatenate([top, low], axis=0)


def kernel(dims, x_hbm, s_hbm, w1_hbm, b_hbm, w2_hbm, t1_hbm, t2_hbm, mt_hbm,
           gin_hbm, g1_hbm, g2_hbm,
           x_v, s_v, w1_v, b_v, w2_v, t1_v, t2_v, mt_v,
           psend, precv, z_v, act, slope, gsc, dz_v, ds_v, qsend, qrecv, gin_v,
           gbuf, drecv, zbufs, zrecvs, g1_v, g2_v,
           in_sem, out_sem, ps_sem, pr_sem, qs_sem, qr_sem, ds_sem, dr_sem, zs_sem, zr_sem):
    n, m, count, block, length_x, pencil, rows = (
        dims["n"], dims["m"], dims["count"], dims["block"],
        dims["length_x"], dims["pencil"], dims["rows"])
    me = lax.axis_index("space")
    mq = lax.axis_index("dp")
    hops = sorted(range(1, n), key=lambda k: abs(k - n / 2))

    line = dims["line"]
    full = 2 * pencil
    short = full - line
    head = full - 2 * line

    def special(shard):
        return lax.rem(shard, n // 2) == 0

    def exchange(send, recv, send_sems, recv_sems, b, k, size):
        peer = lax.rem(me + k, n)
        return pltpu.make_async_remote_copy(
            src_ref=send.at[b, peer, 0:size], dst_ref=recv.at[b, me, 0:size],
            send_sem=send_sems.at[b, k - 1], recv_sem=recv_sems.at[b, k - 1],
            device_id={"space": peer}, device_id_type=MESH)

    def guarded(mirrored, act_on):
        @pl.when(mirrored)
        def _():
            act_on(short)

        @pl.when(jnp.logical_not(mirrored))
        def _():
            act_on(full)

    def first_exchange(b, k, size):
        return exchange(psend, precv, ps_sem, pr_sem, b, k, size)

    def second_exchange(b, k, size):
        return exchange(qsend, qrecv, qs_sem, qr_sem, b, k, size)

    loads = [pltpu.make_async_copy(src, dst, in_sem.at[i]) for i, (src, dst) in enumerate(
        [(t1_hbm, t1_v), (x_hbm, x_v), (s_hbm, s_v), (w1_hbm, w1_v), (b_hbm, b_v),
         (w2_hbm, w2_v), (t2_hbm, t2_v), (mt_hbm, mt_v)])]
    for load in loads[:2]:
        load.start()

    barrier = pltpu.get_barrier_semaphore()
    for k in range(1, n):
        pl.semaphore_signal(barrier, inc=1, device_id={"space": lax.rem(me + k, n)}, device_id_type=MESH)
    for k in range(1, m):
        pl.semaphore_signal(barrier, inc=1, device_id={"dp": lax.rem(mq + k, m)}, device_id_type=MESH)

    for b in range(count):
        for d in range(0, n, n // 2):
            qrecv[b, d, short:full, :] = jnp.zeros((line, block), bf16)
    for load in loads[2:]:
        load.start()
    loads[0].wait()
    loads[1].wait()
    sends = []
    for b in range(count):
        lanes = slice(b * block, (b + 1) * block)
        psend[b] = dot(t1_v[...], x_v[:, lanes], 1, 0).astype(bf16).reshape(psend.shape[1:])
        if b == 0:
            pl.semaphore_wait(barrier, n - 1 + m - 1)
        for k in hops:
            guarded(special(lax.rem(me + k, n)), lambda size: first_exchange(b, k, size).start())
        precv[b, me] = psend[b, me]

    loads[2].wait()
    loads[3].wait()
    loads[4].wait()
    bias = b_v[...].astype(f32)
    total = length_x * pencil
    tile = math.gcd(total, 32)

    def activate(b):
        lanes = slice(b * block, (b + 1) * block)
        w1 = stacked(w1_v[b, 0], w1_v[b, 1])
        pair = jnp.concatenate([s_v[0, :, lanes], s_v[1, :, lanes]], axis=1)
        z_v[...] = dot(pair, w1, 1, 0) + jnp.concatenate([bias[0:1, lanes], bias[1:2, lanes]], axis=1)

        def gelu(t, carry, b=b):
            at = pl.ds(pl.multiple_of(t * tile, tile), tile)
            z = z_v[at, :]
            cdf = 0.5 * (1.0 + lax.erf(z * inv_root_two))
            act[b, at, :] = (z * cdf).astype(bf16)
            slope[b, at, :] = cdf + z * jnp.exp(-0.5 * z * z) * inv_root_tau
            return carry

        lax.fori_loop(0, total // tile, gelu, 0)

    levels = len(zbufs) - 1

    def drecv_copy(b, k):
        peer = lax.rem(mq + k, m)
        return pltpu.make_async_remote_copy(
            src_ref=gbuf.at[peer, b], dst_ref=drecv.at[k - 1, b],
            send_sem=ds_sem.at[b, k - 1], recv_sem=dr_sem.at[b, k - 1],
            device_id={"dp": peer}, device_id_type=MESH)

    def level_copy(b, j):
        half = n >> (j + 1)
        bit = lax.rem(me // (1 << j), 2)
        return pltpu.make_async_remote_copy(
            src_ref=zbufs[j].at[b, pl.ds((1 - bit) * half, half)], dst_ref=zrecvs[j].at[b],
            send_sem=zs_sem.at[b, j], recv_sem=zr_sem.at[b, j],
            device_id={"space": me + (1 - 2 * bit) * (1 << j)}, device_id_type=MESH)

    def fold_gradient(b, j):
        if j == 0:
            for k in range(1, m):
                drecv_copy(b, k).wait_recv()
            for s in range(n):
                value = gbuf[mq, b, s].astype(f32)
                for k in range(1, m):
                    value = value + drecv[k - 1, b, s].astype(f32)
                zbufs[0][b, s] = value.astype(zbufs[0].dtype)
        else:
            level_copy(b, j - 1).wait_recv()
            half = n >> j
            bit = lax.rem(me // (1 << (j - 1)), 2)
            for s in range(half):
                value = zbufs[j - 1][b, bit * half + s].astype(f32) + zrecvs[j - 1][b, s].astype(f32)
                zbufs[j][b, s] = value.astype(zbufs[j].dtype)
        if j < levels:
            copy = level_copy(b, j)
            copy.start()
            sends.append(copy)

    places = [(head, short)] + [
        (k * line, head // 2 + k * line) for k in range(pencil // line - 1)]
    loads[5].wait()
    loads[7].wait()
    activate(0)
    for b in range(count):
        lanes = slice(b * block, (b + 1) * block)
        for k in range(1, n):
            guarded(special(me), lambda size: first_exchange(b, k, size).wait_recv())

        @pl.when(special(me))
        def _():
            for x in range(length_x):
                spread = dot(mt_v[...], precv[b, x, head:short, :], 1, 0)
                precv[b, x, head:full, :] = spread.astype(bf16)

        for r in range(0, pencil, line):
            re_at, im_at = places[r // line]
            planes = [(precv[b, x, re_at:re_at + line, :].astype(f32),
                       precv[b, x, im_at:im_at + line, :].astype(f32)) for x in range(length_x)]
            for kx, (re, im) in enumerate(transform(planes, -1.0)):
                at = slice(kx * pencil + r, kx * pencil + r + line)
                gsc[at, 0:block] = (re * dims["forward_scale"]).astype(bf16)
                gsc[at, block:2 * block] = (im * dims["forward_scale"]).astype(bf16)
        grad = gsc[...]
        w1 = stacked(w1_v[b, 0], w1_v[b, 1])
        w2 = stacked(w2_v[b, 0], w2_v[b, 1])
        dz = (dot(grad, w2, 1, 1) * slope[b]).astype(bf16)
        dz_v[...] = dz
        ds_v[...] = dot(dz, w1, 1, 1)
        for r in range(0, pencil, line):
            re_at, im_at = places[r // line]
            freqs = [(ds_v[kx * pencil + r:kx * pencil + r + line, 0:block],
                      ds_v[kx * pencil + r:kx * pencil + r + line, block:2 * block]) for kx in range(length_x)]
            for x, (re, im) in enumerate(transform(freqs, 1.0)):
                qsend[b, x, re_at:re_at + line, :] = re.astype(bf16)
                qsend[b, x, im_at:im_at + line, :] = im.astype(bf16)

        @pl.when(special(me))
        def _():
            for x in range(length_x):
                merged = dot(mt_v[...], qsend[b, x, head:full, :], 0, 0)
                qsend[b, x, head:short, :] = merged.astype(bf16)

        def pass_on():
            for k in hops:
                guarded(special(me), lambda size: second_exchange(b, k, size).start())
            qrecv[b, me] = qsend[b, me]
            if b + 1 < count:
                activate(b + 1)


        if b + 1 < count:
            pass_on()
        pair = jnp.concatenate([s_v[0, :, lanes], s_v[1, :, lanes]], axis=1)
        for w, (left, right) in enumerate([(pair, dz_v[...]), (act[b], gsc[...])]):
            outer = dot(left, right, 0, 0) * dims["grad_scale"]
            real = outer[:block, :block] + outer[block:, block:]
            imag = outer[:block, block:] - outer[block:, :block]
            for part, value in enumerate([real, imag]):
                for s in range(n):
                    for q in range(m):
                        at = (s * m + q) * rows
                        gbuf[q, b, reverse(s, levels), w, part] = value[at:at + rows].astype(gbuf.dtype)
        for k in range(1, m):
            copy = drecv_copy(b, k)
            copy.start()
            sends.append(copy)
        if b + 1 == count:
            pass_on()
        for j in range(min(b, levels)):
            fold_gradient(b - 1 - j, j)

    for b in range(count, count + levels + 1):
        for j in range(levels + 1):
            if 0 <= b - 1 - j < count and j < levels:
                fold_gradient(b - 1 - j, j)
    outs = []
    loads[6].wait()
    for b in range(count):
        lanes = slice(b * block, (b + 1) * block)
        for k in range(1, n):
            guarded(special(lax.rem(me + n - k, n)), lambda size: second_exchange(b, k, size).wait_recv())
        field = dot(t2_v[...], qrecv[b].reshape(t2_v.shape[1], block), 1, 0)
        gin_v[:, lanes] = (field * dims["inverse_scale"]).astype(bf16)
        copy = pltpu.make_async_copy(gin_v.at[:, lanes], gin_hbm.at[:, lanes], out_sem.at[b])
        copy.start()
        outs.append(copy)
    for b in range(count):
        fold_gradient(b, levels)
        g1_v[b] = zbufs[levels][b, 0, 0].astype(f32)
        g2_v[b] = zbufs[levels][b, 0, 1].astype(f32)
    for i, (src, dst) in enumerate([(g1_v, g1_hbm), (g2_v, g2_hbm)]):
        copy = pltpu.make_async_copy(src, dst, out_sem.at[count + i])
        copy.start()
        outs.append(copy)
    for copy in sends:
        copy.wait_send()
    for b in range(count):
        for k in range(1, n):
            guarded(special(lax.rem(me + k, n)), lambda size: first_exchange(b, k, size).wait_send())
            guarded(special(me), lambda size: second_exchange(b, k, size).wait_send())
    for copy in outs:
        copy.wait()


def body(n, m, grad_out, saved_spectrum, w_first, bias_first, w_second):
    samples, planes, length_y, length_z, width = grad_out.shape
    count, _, block, _ = w_first.shape
    assert samples == 1 and planes == 1
    length_x = planes * n
    cells = length_x * length_y * length_z
    pencil = length_y // n * length_z
    area = length_y * length_z
    total = length_x * pencil
    rows = block // (n * m)
    factor, table = scaled_table(plane_table(length_y, length_z, n))
    norm = 1.0 / math.sqrt(cells)
    dims = dict(n=n, m=m, count=count, block=block, length_x=length_x, pencil=pencil, rows=rows, line=length_z,
                forward_scale=norm / factor, inverse_scale=norm / factor,
                grad_scale=1.0 / math.sqrt(cells * samples * m))
    levels = n.bit_length() - 1
    assert n == 1 << levels
    kept = bf16 if rows % 16 == 0 else f32
    vmem = pltpu.VMEM
    dma = pltpu.SemaphoreType.DMA
    chunk = (2 * pencil, block)
    term = (2, 2, rows, block)
    any_spec = pl.BlockSpec(memory_space=pl.ANY)
    grad_in, grad_first, grad_second = pl.pallas_call(
        functools.partial(kernel, dims),
        out_shape=(
            jax.ShapeDtypeStruct((area, width), bf16),
            jax.ShapeDtypeStruct((count, 2, rows, block), f32),
            jax.ShapeDtypeStruct((count, 2, rows, block), f32),
        ),
        in_specs=[any_spec] * 8,
        out_specs=(any_spec,) * 3,
        scratch_shapes=[
            vmem((area, width), bf16), vmem((2, total, width), bf16), vmem(w_first.shape, bf16),
            vmem(bias_first.shape, bf16), vmem(w_second.shape, bf16),
            vmem(table.shape, bf16), vmem(table.shape[::-1], bf16), vmem((2 * length_z, length_z), bf16),
            vmem((count, n) + chunk, bf16), vmem((count, n) + chunk, bf16),
            vmem((total, 2 * block), f32), vmem((count, total, 2 * block), bf16),
            vmem((count, total, 2 * block), f32), vmem((total, 2 * block), bf16),
            vmem((total, 2 * block), bf16), vmem((total, 2 * block), f32),
            vmem((count, n) + chunk, bf16), vmem((count, n) + chunk, bf16), vmem((area, width), bf16),
            vmem((m, count, n) + term, kept), vmem((max(m - 1, 1), count, n) + term, kept),
            tuple(vmem((count, n >> j) + term, kept if j < levels else f32) for j in range(levels + 1)),
            tuple(vmem((count, max(n >> (j + 1), 1)) + term, kept) for j in range(levels)),
            vmem((count, 2, rows, block), f32), vmem((count, 2, rows, block), f32),
            dma((8,)), dma((count + 2,)),
            dma((count, n)), dma((count, n)), dma((count, n)), dma((count, n)),
            dma((count, m)), dma((count, m)), dma((count, n)), dma((count, n)),
        ],
        compiler_params=pltpu.CompilerParams(collective_id=0, has_side_effects=True),
        name="mixer",
    )(
        grad_out.reshape(area, width), saved_spectrum.reshape(2, total, width), w_first, bias_first, w_second,
        jnp.asarray(table), jnp.asarray(np.ascontiguousarray(table.T)),
        jnp.asarray(mirror_table(length_z).astype(ml_dtypes.bfloat16)),
    )
    def place(a, b, c, d, e, f, a_v, b_v, c_v, in_sem, out_sem):
        quarter = area // 4
        moves = [(b, b_v, e), (c, c_v, f)] + [
            (a.at[i * quarter:(i + 1) * quarter], a_v.at[i * quarter:(i + 1) * quarter], d.at[i * quarter:(i + 1) * quarter])
            for i in range(4)]
        loads = [pltpu.make_async_copy(x, y, in_sem.at[i]) for i, (x, y, _) in enumerate(moves)]
        stores = [pltpu.make_async_copy(y, z, out_sem.at[i]) for i, (_, y, z) in enumerate(moves)]
        for load in loads:
            load.start()
        for load, store in zip(loads, stores):
            load.wait()
            store.start()
        for store in stores:
            store.wait()

    grad_in, grad_first, grad_second = pl.pallas_call(
        place,
        out_shape=tuple(jax.ShapeDtypeStruct(a.shape, a.dtype) for a in (grad_in, grad_first, grad_second)),
        in_specs=[any_spec] * 3, out_specs=(any_spec,) * 3,
        scratch_shapes=[vmem(a.shape, a.dtype) for a in (grad_in, grad_first, grad_second)] + [dma((6,)), dma((6,))],
        name="place",
    )(grad_in, grad_first, grad_second)
    return (grad_in.reshape(grad_out.shape), grad_first, grad_second)


def solution(mesh):
    in_specs = (
        P(("parts", "dp"), "space", None, None, "chan"),
        P(None, ("parts", "dp"), None, "space", None, "chan"),
        P("chan", None, None, None),
        P(None, "chan"),
        P("chan", None, None, None),
    )
    out_specs = (
        P(("parts", "dp"), "space", None, None, "chan"),
        P(("parts", "chan"), None, ("space", "dp"), None),
        P(("parts", "chan"), None, ("space", "dp"), None),
    )
    local = functools.partial(body, mesh.shape["space"], mesh.shape["dp"])
    return jax.shard_map(local, mesh=mesh, in_specs=in_specs, out_specs=out_specs, check_vma=False)
```
